32 devices in a mesh: ctx: 4 (over y, x), head: 8 (over z, core).
Axes of the slice: x: 2, y: 2, z: 4, core: 2. Of those that a mesh axis runs over, the one named last changes fastest.
Arguments:
- query_rows: bfloat16 [4096, 8192], P('ctx', 'head'), may hold values from -6 to 6
- key_rows: bfloat16 [4096, 8192], P('ctx', 'head'), may hold values from -6 to 6
- value_rows: bfloat16 [4096, 8192], P('ctx', 'head'), may hold values from -6 to 6
- decay_rate: float32 [64], P('head'), as said below
- starts: int32 [4096], P('ctx'), may hold values 0 or 1
- norm_gain: float32 [8192], P('head'), may hold values from 0.1 to 1.9
- grad_out: bfloat16 [4096, 8192], P('ctx', 'head'), may hold values from -6 to 6
Outputs:
- normed: bfloat16 [4096, 8192], P('ctx', 'head')
- grad_query: bfloat16 [4096, 8192], P('ctx', 'head')
- grad_key: bfloat16 [4096, 8192], P('ctx', 'head')
- grad_value: bfloat16 [4096, 8192], P('ctx', 'head')
The draws below stay inside these ranges and needn't reach their ends.
Inputs may be any that keep to these rules, and one draw needn't show every extreme that they name: `decay_rate`: positive rates; a head keeps exp(-rate) of its state per position. `starts`: 1 where a document begins, 0 elsewhere.
All inputs are finite; a program needn't handle non-finite values. No bound on the sum of `starts` on one device may be relied on, other than what follows from the above.
Results may differ from the reference program's by a relative error of at most 0.008.
Values sent between devices are 32-bit elements; how exact they have to be, the bound alone decides.
A program may use at most 128 MiB of HBM per device.

```python
import math
import jax
import jax.numpy as jnp
from jax import lax

HEADS = 64
DH = 128
TOK_DEV = 1024
BLOCK = 512
TOKENS = 4096


def draw_decay_rate(key, part):
    pick_key, fast_key, slow_key = jax.random.split(key, 3)
    share = 0.5
    chosen = jax.random.uniform(pick_key, (HEADS,)) < share
    fast = jnp.exp(jax.random.uniform(fast_key, (HEADS,), minval=math.log(1.0 / 50.0), maxval=math.log(1.0 / 15.0)))
    slow = jnp.exp(jax.random.uniform(slow_key, (HEADS,), minval=math.log(0.2 / TOKENS), maxval=math.log(2.2 / TOKENS)))
    return jnp.where(chosen, fast, slow).astype(jnp.float32)


def touch_ends(drawn, stream_key, least, top_value):
    longest = drawn.shape.index(max(drawn.shape))
    spots = []
    for shift in (0, 1):
        where = [jax.random.randint(jax.random.fold_in(stream_key, axis), (), 0, length) for axis, length in enumerate(drawn.shape)]
        where[longest] = (where[longest] + shift) % drawn.shape[longest]
        spots.append(tuple(where))
    return drawn.at[spots[0]].set(least).at[spots[1]].set(top_value)


def shard_levels(stream_key, dims, shards, least, high):
    factor_of, own = 1.0, jax.random.fold_in(stream_key, 6)
    for dim, blocks in shards:
        heights = jnp.exp(jax.random.uniform(jax.random.fold_in(own, dim), (blocks,), jnp.float32, least / len(shards), high / len(shards)))
        factor_of = factor_of * jnp.repeat(heights, dims[dim] // blocks).reshape([-1 if axis == dim else 1 for axis in range(len(dims))])
    return factor_of


def normal_values(key, shape, scale, most, cuts=(), dtype=jnp.bfloat16):
    result = scale * jax.random.normal(key, shape, jnp.float32)
    if cuts:
        result = result * shard_levels(key, shape, cuts, -0.22, 0.18)
    return jnp.clip(result, -most, most).astype(dtype)


def setup_inputs(seed: int = 0) -> dict:
    streams_of = jax.random.split(jax.random.key(seed), 8)
    query_rows = normal_values(streams_of[0], (TOKENS, HEADS * DH), 1.0, 6.0, ((0, 4), (1, 8)))
    key_rows = normal_values(streams_of[1], (TOKENS, HEADS * DH), 1.0, 6.0, ((0, 4), (1, 8)))
    value_rows = normal_values(streams_of[2], (TOKENS, HEADS * DH), 1.0, 6.0, ((0, 4), (1, 8)))
    decay_rate = draw_decay_rate(jax.random.fold_in(streams_of[7], 71), 0)
    starts = touch_ends((jax.random.randint(streams_of[4], (TOKENS,), 0, 8 * TOK_DEV) < 1).astype(jnp.int32), jax.random.fold_in(streams_of[4], 1), 0, 1)
    norm_gain = jnp.clip(1.0 + 0.18 * jax.random.normal(streams_of[5], (HEADS * DH,), jnp.float32), 0.1, 1.9)
    grad_out = normal_values(streams_of[6], (TOKENS, HEADS * DH), 1.0, 6.0, ((0, 4), (1, 8)))
    return dict(query_rows=query_rows, key_rows=key_rows, value_rows=value_rows, decay_rate=decay_rate, starts=starts, norm_gain=norm_gain, grad_out=grad_out)


HIGH = lax.Precision.HIGHEST
EPSILON = 1e-06

def block_masks(flags, rates, width):
    running = jnp.cumsum(flags).astype(jnp.int32)
    place = jnp.arange(width).astype(jnp.float32)
    offset = place[:, None] - place[None, :]
    joined = (running[:, None] == running[None, :]) & (offset >= 0.0)
    decay_mask = jnp.where(joined[None], jnp.exp(-rates[:, None, None] * jnp.maximum(offset, 0.0)[None]), 0.0)
    reach_in = jnp.where((running == 0)[None], jnp.exp(-rates[:, None] * (place + 1.0)[None]), 0.0)
    reach_out = jnp.where((running == running[-1])[None], jnp.exp(-rates[:, None] * (width - 1.0 - place)[None]), 0.0)
    carry_over = jnp.where(running[-1] == 0, jnp.exp(-rates * width), 0.0)
    return (decay_mask, reach_in, reach_out, carry_over)

def reference(query_rows, key_rows, value_rows, decay_rate, starts, norm_gain, grad_out):
    blocks = TOKENS // BLOCK
    layout = (blocks, BLOCK, HEADS, DH)
    query_blocks = query_rows.reshape(layout)
    key_blocks = key_rows.reshape(layout)
    value_blocks = value_rows.reshape(layout)
    flag_blocks = starts.reshape(blocks, BLOCK)

    def forward_step(state, inputs):
        query_block, key_block, value_block, flags = inputs
        decay_mask, reach_in, reach_out, carry_over = block_masks(flags, decay_rate, BLOCK)
        query_wide = query_block.astype(jnp.float32)
        key_wide = key_block.astype(jnp.float32)
        value_wide = value_block.astype(jnp.float32)
        scores = jnp.einsum('thd,shd->hts', query_wide, key_wide, precision=HIGH)
        weights = lax.optimization_barrier((scores * decay_mask).astype(jnp.bfloat16)).astype(jnp.float32)
        local_out = jnp.einsum('hts,she->the', weights, value_wide, precision=HIGH)
        carried = jnp.transpose(reach_in)[:, :, None] * jnp.einsum('thd,hde->the', query_wide, state, precision=HIGH)
        weighted_keys = key_wide * jnp.transpose(reach_out)[:, :, None]
        new_state = carry_over[:, None, None] * state + jnp.einsum('shd,she->hde', weighted_keys, value_wide, precision=HIGH)
        return (new_state, (local_out + carried, state))
    zero_state = jnp.zeros((HEADS, DH, DH), jnp.float32)
    last_state, (attended, before) = lax.scan(forward_step, zero_state, (query_blocks, key_blocks, value_blocks, flag_blocks))
    outputs = attended.reshape(TOKENS, HEADS * DH)
    inverse = 1.0 / jnp.sqrt(lax.optimization_barrier(jnp.mean(outputs * outputs, axis=1)) + EPSILON)
    normed = (outputs * inverse[:, None] * norm_gain[None, :]).astype(jnp.bfloat16)
    gained = grad_out.astype(jnp.float32) * norm_gain[None, :]
    cross = lax.optimization_barrier(jnp.mean(gained * outputs, axis=1))
    grad_att = (inverse[:, None] * gained - outputs * (inverse * inverse * inverse * cross)[:, None]).astype(jnp.bfloat16)
    grad_blocks = grad_att.reshape(layout)

    def backward_step(later, inputs):
        query_block, key_block, value_block, flags, grad_block, state = inputs
        decay_mask, reach_in, reach_out, carry_over = block_masks(flags, decay_rate, BLOCK)
        query_wide = query_block.astype(jnp.float32)
        key_wide = key_block.astype(jnp.float32)
        value_wide = value_block.astype(jnp.float32)
        grad_wide = grad_block.astype(jnp.float32)
        scores = jnp.einsum('thd,shd->hts', query_wide, key_wide, precision=HIGH)
        weights = lax.optimization_barrier((scores * decay_mask).astype(jnp.bfloat16)).astype(jnp.float32)
        grad_weights = jnp.einsum('the,she->hts', grad_wide, value_wide, precision=HIGH)
        grad_scores = lax.optimization_barrier((grad_weights * decay_mask).astype(jnp.bfloat16)).astype(jnp.float32)
        grad_query = jnp.einsum('hts,shd->thd', grad_scores, key_wide, precision=HIGH)
        grad_query = grad_query + jnp.transpose(reach_in)[:, :, None] * jnp.einsum('the,hde->thd', grad_wide, state, precision=HIGH)
        grad_key = jnp.einsum('hts,thd->shd', grad_scores, query_wide, precision=HIGH)
        grad_key = grad_key + jnp.transpose(reach_out)[:, :, None] * jnp.einsum('she,hde->shd', value_wide, later, precision=HIGH)
        grad_value = jnp.einsum('hts,the->she', weights, grad_wide, precision=HIGH)
        grad_value = grad_value + jnp.transpose(reach_out)[:, :, None] * jnp.einsum('shd,hde->she', key_wide, later, precision=HIGH)
        earlier = carry_over[:, None, None] * later + jnp.einsum('thd,the->hde', query_wide * jnp.transpose(reach_in)[:, :, None], grad_wide, precision=HIGH)
        return (earlier, (grad_query.astype(jnp.bfloat16), grad_key.astype(jnp.bfloat16), grad_value.astype(jnp.bfloat16)))
    first_grad, (grad_query, grad_key, grad_value) = lax.scan(backward_step, zero_state, (query_blocks, key_blocks, value_blocks, flag_blocks, grad_blocks, before), reverse=True)
    shape_out = (TOKENS, HEADS * DH)
    return (normed, grad_query.reshape(shape_out), grad_key.reshape(shape_out), grad_value.reshape(shape_out))
```

```python
import functools

import jax
import jax.numpy as jnp
from jax import lax
from jax.experimental import pallas as pl
from jax.experimental.pallas import tpu as pltpu
from jax.sharding import PartitionSpec as P

HEADS = 64
DH = 128
CHUNK = 256
EPSILON = 1e-06
MESH = pl.DeviceIdType.MESH
F32 = jnp.float32
BF16 = jnp.bfloat16


def dot(a, b, da, db):
    return lax.dot_general(a, b, (((da,), (db,)), ((), ())), preferred_element_type=F32)


def kernel(
    steps, peers, total,
    q_hbm, k_hbm, v_hbm, g_hbm, rate_ref, starts_ref, gain_ref,
    n_out, gq_out, gk_out, gv_out,
    qs, ks, vs, gs, att, ga, weights, gkp, gvp, ns, gqs, gks, gvs,
    joined, in_mask, out_mask, clear, d_state, full_state, d_grad,
    own, got, pre, sq_acc, cr_acc, inv_full, coef_full, x_buf,
    in_sem, out_sem, s_send, s_recv, x_send, x_recv,
):
    heads, rows, _ = qs.shape
    chunks = rows // CHUNK
    ctx = lax.axis_index("ctx")
    me = lax.axis_index("head")

    def cols(h):
        return pl.ds(pl.multiple_of(h * DH, DH), DH)

    def load(i, h):
        hbm, buf = ((k_hbm, ks), (v_hbm, vs), (q_hbm, qs), (g_hbm, gs))[i]
        return pltpu.make_async_copy(hbm.at[:, cols(h)], buf.at[h], in_sem.at[i, h])

    def store(i, h):
        buf, hbm = ((ns, n_out), (gqs, gq_out), (gks, gk_out), (gvs, gv_out))[i]
        return pltpu.make_async_copy(buf.at[h], hbm.at[:, cols(h)], out_sem.at[i, h])

    def partner(step):
        size = 1 << step
        bit = (ctx // size) % 2
        return bit, ctx + size - 2 * size * bit

    def scan_copy(which, step, h):
        return pltpu.make_async_remote_copy(
            src_ref=own.at[which, step, h],
            dst_ref=got.at[which, step, h],
            send_sem=s_send.at[which, step, h],
            recv_sem=s_recv.at[which, step, h],
            device_id=(partner(step)[1], me),
            device_id_type=MESH,
        )

    def swap_copy(k):
        return pltpu.make_async_remote_copy(
            src_ref=x_buf.at[0],
            dst_ref=x_buf.at[k],
            send_sem=x_send.at[k],
            recv_sem=x_recv.at[k],
            device_id=(ctx, (me + k) % peers),
            device_id_type=MESH,
        )

    def start_loads(pair):
        def go(h, c):
            for i in pair:
                load(i, h).start()
            return c
        lax.fori_loop(0, heads, go, 0)

    start_loads((0, 1))
    start_loads((2, 3))

    barrier = pltpu.get_barrier_semaphore()
    for step in range(steps):
        pl.semaphore_signal(barrier, inc=1, device_id=(partner(step)[1], me), device_id_type=MESH)

    def greet(k, c):
        pl.semaphore_signal(
            barrier, inc=1, device_id=(ctx, (me + k) % peers), device_id_type=MESH
        )
        return c

    lax.fori_loop(1, peers, greet, 0)

    row_at = lax.broadcasted_iota(jnp.int32, (CHUNK, CHUNK), 0)
    col_at = lax.broadcasted_iota(jnp.int32, (CHUNK, CHUNK), 1)
    lower = row_at >= col_at
    ones_low = jnp.where(lower, 1.0, 0.0).astype(BF16)
    for c in range(chunks):
        flags = starts_ref[:, c * CHUNK:(c + 1) * CHUNK].astype(F32)
        wide = jnp.broadcast_to(flags, (DH, CHUNK)).astype(BF16)
        run_row = dot(wide, ones_low, 1, 1)[0:1, :]
        run_col = dot(ones_low, wide, 1, 1)
        count = jnp.sum(flags, axis=1, keepdims=True)
        both = jnp.concatenate([run_col] * (CHUNK // DH), axis=1)
        joined[c] = jnp.where(lower & (both == run_row), 1.0, 0.0)
        in_mask[c] = jnp.where(run_col == 0.0, 1.0, 0.0)
        out_mask[c] = jnp.where(run_col == count, 1.0, 0.0)
        clear[c] = jnp.broadcast_to(jnp.where(count == 0.0, 1.0, 0.0), (8, DH))
    sq_acc[...] = jnp.zeros_like(sq_acc)
    cr_acc[...] = jnp.zeros_like(cr_acc)

    place = lax.broadcasted_iota(jnp.int32, (CHUNK, DH), 0).astype(F32)
    gap = jnp.maximum(row_at - col_at, 0).astype(F32)

    def reach_in(rate):
        return jnp.exp(-rate * (place + 1.0))

    def reach_out(rate):
        return jnp.exp(-rate * (CHUNK - 1.0 - place))

    def carry(rate, c):
        return clear[c] * jnp.exp(jnp.full((8, DH), -rate * CHUNK, F32))

    def put(which, step, h, state, factor):
        own[which, step, h, 0:DH, :] = state
        own[which, step, h, DH:DH + 8, :] = factor

    def take(which, step, h, want_total):
        scan_copy(which, step, h).wait_recv()
        bit, _ = partner(step)
        ahead = (bit == 1) if which == 0 else (bit == 0)
        came, came_f = got[which, step, h, 0:DH, :], got[which, step, h, DH:DH + 8, :]
        if step == 0:
            state = jnp.where(ahead, came, 0.0)
            factor = jnp.where(ahead, came_f, 1.0)
        else:
            old, old_f = pre[h, 0:DH, :], pre[h, DH:DH + 8, :]
            state = jnp.where(ahead, old_f[0:1, :] * came + old, old)
            factor = jnp.where(ahead, old_f * came_f, old_f)
        if not want_total:
            return state
        pre[h, 0:DH, :] = state
        pre[h, DH:DH + 8, :] = factor
        mine, mine_f = own[which, step, h, 0:DH, :], own[which, step, h, DH:DH + 8, :]
        merged = jnp.where(ahead, mine_f[0:1, :] * came + mine, came_f[0:1, :] * mine + came)
        put(which, step + 1, h, merged, mine_f * came_f)
        scan_copy(which, step + 1, h).start()
        return None

    def part(c):
        return slice(c * CHUNK, (c + 1) * CHUNK)

    pl.semaphore_wait(barrier, steps + peers - 1)

    def make_states(h, carried):
        load(0, h).wait()
        load(1, h).wait()
        rate = rate_ref[h]
        out = reach_out(rate)
        state = jnp.zeros((DH, DH), F32)
        factor = jnp.ones((8, DH), F32)
        for c in range(chunks):
            weighted = (ks[h, part(c), :].astype(F32) * (out * out_mask[c])).astype(BF16)
            add = dot(weighted, vs[h, part(c), :], 0, 0)
            d_state[h, c] = add
            keep = carry(rate, c)
            state = keep[0:1, :] * state + add
            factor = factor * keep
        put(0, 0, h, state, factor)
        scan_copy(0, 0, h).start()
        return carried

    lax.fori_loop(0, heads, make_states, 0)

    def attend(h, carried):
        load(2, h).wait()
        load(3, h).wait()
        decay = jnp.exp(-rate_ref[h] * gap)
        for c in range(chunks):
            scores = dot(qs[h, part(c), :], ks[h, part(c), :], 1, 1)
            w = (scores * (decay * joined[c])).astype(BF16)
            weights[h, c] = w
            att[h, part(c), :] = dot(w, vs[h, part(c), :], 1, 0)
        for step in range(steps - 1):
            take(0, step, h, True)
        return carried

    lax.fori_loop(0, heads, attend, 0)

    def finish_attend(h, carried):
        rate = rate_ref[h]
        state = take(0, steps - 1, h, False)
        reach = reach_in(rate)
        gain = gain_ref[pl.ds(h, 1), :]
        for c in range(chunks):
            small = state.astype(BF16)
            full_state[h, c] = small
            a = att[h, part(c), :] + (reach * in_mask[c]) * dot(qs[h, part(c), :], small, 1, 0)
            att[h, part(c), :] = a
            sq_acc[part(c), :] += a * a
            cr_acc[part(c), :] += gs[h, part(c), :].astype(F32) * gain * a
            if c < chunks - 1:
                state = carry(rate, c)[0:1, :] * state + d_state[h, c]
        return carried

    lax.fori_loop(0, heads, finish_attend, 0)

    x_buf[0, 0:1, :] = jnp.sum(jnp.transpose(sq_acc[...]), axis=0, keepdims=True)
    x_buf[0, 1:2, :] = jnp.sum(jnp.transpose(cr_acc[...]), axis=0, keepdims=True)

    def send(k, c):
        swap_copy(k).start()
        return c

    lax.fori_loop(1, peers, send, 0)

    def receive(k, c):
        swap_copy(k).wait_recv()
        return c + x_buf[k]

    sums = lax.fori_loop(1, peers, receive, x_buf[0])
    inverse = 1.0 / jnp.sqrt(sums[0:1, :] / total + EPSILON)
    coef = inverse * inverse * inverse * (sums[1:2, :] / total)
    inv_full[...] = jnp.transpose(jnp.broadcast_to(inverse, (DH, rows)))
    coef_full[...] = jnp.transpose(jnp.broadcast_to(coef, (DH, rows)))

    def make_grads(h, carried):
        rate = rate_ref[h]
        reach = reach_in(rate)
        gain = gain_ref[pl.ds(h, 1), :]
        state = jnp.zeros((DH, DH), F32)
        factor = jnp.ones((8, DH), F32)
        for c in reversed(range(chunks)):
            a, inv = att[h, part(c), :], inv_full[part(c), :]
            ns[h, part(c), :] = (a * inv * gain).astype(BF16)
            gained = gs[h, part(c), :].astype(F32) * gain
            grad = (inv * gained - a * coef_full[part(c), :]).astype(BF16)
            ga[h, part(c), :] = grad
            weighted = (qs[h, part(c), :].astype(F32) * (reach * in_mask[c])).astype(BF16)
            add = dot(weighted, grad, 0, 0)
            d_grad[h, c] = add
            keep = carry(rate, c)
            state = keep[0:1, :] * state + add
            factor = factor * keep
        put(1, 0, h, state, factor)
        scan_copy(1, 0, h).start()
        store(0, h).start()
        return carried

    lax.fori_loop(0, heads, make_grads, 0)

    def inner_grads(h, carried):
        rate = rate_ref[h]
        decay = jnp.exp(-rate * gap)
        reach = reach_in(rate)
        for c in range(chunks):
            grad = ga[h, part(c), :]
            d = (dot(grad, vs[h, part(c), :], 1, 1) * (decay * joined[c])).astype(BF16)
            gq = dot(d, ks[h, part(c), :], 1, 0)
            gq += (reach * in_mask[c]) * dot(grad, full_state[h, c], 1, 1)
            gqs[h, part(c), :] = gq.astype(BF16)
            gkp[h, part(c), :] = dot(d, qs[h, part(c), :], 0, 0)
            gvp[h, part(c), :] = dot(weights[h, c], grad, 0, 0)
        for step in range(steps - 1):
            take(1, step, h, True)
        store(1, h).start()
        return carried

    lax.fori_loop(0, heads, inner_grads, 0)

    def finish_grads(h, carried):
        rate = rate_ref[h]
        state = take(1, steps - 1, h, False)
        out = reach_out(rate)
        for c in reversed(range(chunks)):
            small = state.astype(BF16)
            reach = out * out_mask[c]
            gk = gkp[h, part(c), :] + reach * dot(vs[h, part(c), :], small, 1, 1)
            gv = gvp[h, part(c), :] + reach * dot(ks[h, part(c), :], small, 1, 0)
            gks[h, part(c), :] = gk.astype(BF16)
            gvs[h, part(c), :] = gv.astype(BF16)
            if c > 0:
                state = carry(rate, c)[0:1, :] * state + d_grad[h, c]
        store(2, h).start()
        store(3, h).start()
        return carried

    lax.fori_loop(0, heads, finish_grads, 0)

    def drain(h, carried):
        for which in range(2):
            for step in range(steps):
                scan_copy(which, step, h).wait_send()
        for i in range(4):
            store(i, h).wait()
        return carried

    lax.fori_loop(0, heads, drain, 0)

    def drain_swaps(k, c):
        swap_copy(k).wait_send()
        return c

    lax.fori_loop(1, peers, drain_swaps, 0)


def body(steps, peers, query_rows, key_rows, value_rows, decay_rate, starts, norm_gain, grad_out):
    rows, features = query_rows.shape
    heads = features // DH
    chunks = rows // CHUNK
    big = jax.ShapeDtypeStruct((rows, features), BF16)
    whole = pl.BlockSpec(memory_space=pl.ANY)
    inside = pl.BlockSpec(memory_space=pltpu.VMEM)

    def head_rows(dtype):
        return pltpu.VMEM((heads, rows, DH), dtype)

    dma = pltpu.SemaphoreType.DMA
    return pl.pallas_call(
        functools.partial(kernel, steps, peers, HEADS * DH),
        out_shape=(big,) * 4,
        in_specs=[whole] * 4 + [pl.BlockSpec(memory_space=pltpu.SMEM), inside, inside],
        out_specs=(whole,) * 4,
        scratch_shapes=[head_rows(BF16)] * 4
        + [head_rows(F32), head_rows(BF16), pltpu.VMEM((heads, chunks, CHUNK, CHUNK), BF16)]
        + [head_rows(F32)] * 2
        + [head_rows(BF16)] * 4
        + [
            pltpu.VMEM((chunks, CHUNK, CHUNK), F32),
            pltpu.VMEM((chunks, CHUNK, DH), F32),
            pltpu.VMEM((chunks, CHUNK, DH), F32),
            pltpu.VMEM((chunks, 8, DH), F32),
            pltpu.VMEM((heads, chunks, DH, DH), F32),
            pltpu.VMEM((heads, chunks, DH, DH), BF16),
            pltpu.VMEM((heads, chunks, DH, DH), F32),
            pltpu.VMEM((2, steps, heads, DH + 8, DH), F32),
            pltpu.VMEM((2, steps, heads, DH + 8, DH), F32),
            pltpu.VMEM((heads, DH + 8, DH), F32),
            pltpu.VMEM((rows, DH), F32),
            pltpu.VMEM((rows, DH), F32),
            pltpu.VMEM((rows, DH), F32),
            pltpu.VMEM((rows, DH), F32),
            pltpu.VMEM((peers, 2, rows), F32),
            dma((4, heads)),
            dma((4, heads)),
            dma((2, steps, heads)),
            dma((2, steps, heads)),
            dma((peers,)),
            dma((peers,)),
        ],
        compiler_params=pltpu.CompilerParams(
            collective_id=0, has_side_effects=True, vmem_limit_bytes=60 * 1024 * 1024
        ),
    )(
        query_rows, key_rows, value_rows, grad_out, decay_rate,
        starts.reshape(1, rows), norm_gain.reshape(heads, DH),
    )


def solution(mesh):
    steps = (mesh.shape["ctx"] - 1).bit_length()
    both = P("ctx", "head")
    return jax.shard_map(
        functools.partial(body, steps, mesh.shape["head"]),
        mesh=mesh,
        in_specs=(both, both, both, P("head"), P("ctx"), P("head"), both),
        out_specs=(both,) * 4,
        check_vma=False,
    )
```

```python
import functools

import jax
import jax.numpy as jnp
from jax import lax
from jax.experimental import pallas as pl
from jax.experimental.pallas import tpu as pltpu
from jax.sharding import PartitionSpec as P

HEADS = 64
DH = 128
CHUNK = 256
EPSILON = 1e-06
MESH = pl.DeviceIdType.MESH
F32 = jnp.float32
BF16 = jnp.bfloat16


def dot(a, b, da, db):
    return lax.dot_general(a, b, (((da,), (db,)), ((), ())), preferred_element_type=F32)


def kernel(
    steps, peers, total,
    q_hbm, k_hbm, v_hbm, g_hbm, rate_ref, starts_ref, gain_ref,
    n_out, gq_out, gk_out, gv_out,
    qs, ks, vs, gs, att, ga, weights, gkp, gvp,
    joined, in_mask, out_mask, clear, d_state, full_state, d_grad,
    own, got, pre, sq_acc, cr_acc, inv_full, coef_full, x_buf,
    in_sem, s_send, s_recv, x_send, x_recv,
):
    heads, rows, _ = qs.shape
    chunks = rows // CHUNK
    ctx = lax.axis_index("ctx")
    me = lax.axis_index("head")

    def cols(h):
        return pl.ds(pl.multiple_of(h * DH, DH), DH)

    def load(i, h):
        hbm, buf = ((k_hbm, ks), (v_hbm, vs), (q_hbm, qs), (g_hbm, gs))[i]
        return pltpu.make_async_copy(hbm.at[:, cols(h)], buf.at[h], in_sem.at[i, h])

    def partner(step):
        size = 1 << step
        bit = (ctx // size) % 2
        return bit, ctx + size - 2 * size * bit

    def scan_copy(which, step, h):
        return pltpu.make_async_remote_copy(
            src_ref=own.at[which, step, h],
            dst_ref=got.at[which, step, h],
            send_sem=s_send.at[which, step, h],
            recv_sem=s_recv.at[which, step, h],
            device_id=(partner(step)[1], me),
            device_id_type=MESH,
        )

    def swap_copy(k):
        return pltpu.make_async_remote_copy(
            src_ref=x_buf.at[0],
            dst_ref=x_buf.at[k],
            send_sem=x_send.at[k],
            recv_sem=x_recv.at[k],
            device_id=(ctx, (me + k) % peers),
            device_id_type=MESH,
        )

    def start_loads(pair):
        def go(h, c):
            for i in pair:
                load(i, h).start()
            return c
        lax.fori_loop(0, heads, go, 0)

    start_loads((0, 1))
    start_loads((2, 3))

    barrier = pltpu.get_barrier_semaphore()
    for step in range(steps):
        pl.semaphore_signal(barrier, inc=1, device_id=(partner(step)[1], me), device_id_type=MESH)

    def greet(k, c):
        pl.semaphore_signal(
            barrier, inc=1, device_id=(ctx, (me + k) % peers), device_id_type=MESH
        )
        return c

    lax.fori_loop(1, peers, greet, 0)

    row_at = lax.broadcasted_iota(jnp.int32, (CHUNK, CHUNK), 0)
    col_at = lax.broadcasted_iota(jnp.int32, (CHUNK, CHUNK), 1)
    lower = row_at >= col_at
    ones_low = jnp.where(lower, 1.0, 0.0).astype(BF16)
    for c in range(chunks):
        flags = starts_ref[:, c * CHUNK:(c + 1) * CHUNK].astype(F32)
        wide = jnp.broadcast_to(flags, (DH, CHUNK)).astype(BF16)
        run_row = dot(wide, ones_low, 1, 1)[0:1, :]
        run_col = dot(ones_low, wide, 1, 1)
        count = jnp.sum(flags, axis=1, keepdims=True)
        both = jnp.concatenate([run_col] * (CHUNK // DH), axis=1)
        joined[c] = jnp.where(lower & (both == run_row), 1.0, 0.0)
        in_mask[c] = jnp.where(run_col == 0.0, 1.0, 0.0)
        out_mask[c] = jnp.where(run_col == count, 1.0, 0.0)
        clear[c] = jnp.broadcast_to(jnp.where(count == 0.0, 1.0, 0.0), (8, DH))
    sq_acc[...] = jnp.zeros_like(sq_acc)
    cr_acc[...] = jnp.zeros_like(cr_acc)

    place = lax.broadcasted_iota(jnp.int32, (CHUNK, DH), 0).astype(F32)
    gap = jnp.maximum(row_at - col_at, 0).astype(F32)

    def reach_in(rate):
        return jnp.exp(-rate * (place + 1.0))

    def reach_out(rate):
        return jnp.exp(-rate * (CHUNK - 1.0 - place))

    def carry(rate, c):
        return clear[c] * jnp.exp(jnp.full((8, DH), -rate * CHUNK, F32))

    def put(which, step, h, state, factor):
        own[which, step, h, 0:DH, :] = state
        own[which, step, h, DH:DH + 8, :] = factor

    def take(which, step, h, want_total):
        scan_copy(which, step, h).wait_recv()
        bit, _ = partner(step)
        ahead = (bit == 1) if which == 0 else (bit == 0)
        came, came_f = got[which, step, h, 0:DH, :], got[which, step, h, DH:DH + 8, :]
        if step == 0:
            state = jnp.where(ahead, came, 0.0)
            factor = jnp.where(ahead, came_f, 1.0)
        else:
            old, old_f = pre[h, 0:DH, :], pre[h, DH:DH + 8, :]
            state = jnp.where(ahead, old_f[0:1, :] * came + old, old)
            factor = jnp.where(ahead, old_f * came_f, old_f)
        if not want_total:
            return state
        pre[h, 0:DH, :] = state
        pre[h, DH:DH + 8, :] = factor
        mine, mine_f = own[which, step, h, 0:DH, :], own[which, step, h, DH:DH + 8, :]
        merged = jnp.where(ahead, mine_f[0:1, :] * came + mine, came_f[0:1, :] * mine + came)
        put(which, step + 1, h, merged, mine_f * came_f)
        scan_copy(which, step + 1, h).start()
        return None

    def part(c):
        return slice(c * CHUNK, (c + 1) * CHUNK)

    pl.semaphore_wait(barrier, steps + peers - 1)

    def make_states(h, carried):
        load(0, h).wait()
        load(1, h).wait()
        rate = rate_ref[h]
        out = reach_out(rate)
        state = jnp.zeros((DH, DH), F32)
        factor = jnp.ones((8, DH), F32)
        for c in range(chunks):
            weighted = (ks[h, part(c), :].astype(F32) * (out * out_mask[c])).astype(BF16)
            add = dot(weighted, vs[h, part(c), :], 0, 0)
            d_state[h, c] = add
            keep = carry(rate, c)
            state = keep[0:1, :] * state + add
            factor = factor * keep
        put(0, 0, h, state, factor)
        scan_copy(0, 0, h).start()
        return carried

    lax.fori_loop(0, heads, make_states, 0)

    def attend(h, carried):
        load(2, h).wait()
        load(3, h).wait()
        decay = jnp.exp(-rate_ref[h] * gap)
        for c in range(chunks):
            scores = dot(qs[h, part(c), :], ks[h, part(c), :], 1, 1)
            w = (scores * (decay * joined[c])).astype(BF16)
            weights[h, c] = w
            att[h, part(c), :] = dot(w, vs[h, part(c), :], 1, 0)
        for step in range(steps - 1):
            take(0, step, h, True)
        return carried

    lax.fori_loop(0, heads, attend, 0)

    def finish_attend(h, carried):
        rate = rate_ref[h]
        state = take(0, steps - 1, h, False)
        reach = reach_in(rate)
        gain = gain_ref[pl.ds(h, 1), :]
        for c in range(chunks):
            small = state.astype(BF16)
            full_state[h, c] = small
            a = att[h, part(c), :] + (reach * in_mask[c]) * dot(qs[h, part(c), :], small, 1, 0)
            att[h, part(c), :] = a
            sq_acc[part(c), :] += a * a
            cr_acc[part(c), :] += gs[h, part(c), :].astype(F32) * gain * a
            if c < chunks - 1:
                state = carry(rate, c)[0:1, :] * state + d_state[h, c]
        return carried

    lax.fori_loop(0, heads, finish_attend, 0)

    x_buf[0, 0:1, :] = jnp.sum(jnp.transpose(sq_acc[...]), axis=0, keepdims=True)
    x_buf[0, 1:2, :] = jnp.sum(jnp.transpose(cr_acc[...]), axis=0, keepdims=True)

    def send(k, c):
        swap_copy(k).start()
        return c

    lax.fori_loop(1, peers, send, 0)

    def receive(k, c):
        swap_copy(k).wait_recv()
        return c + x_buf[k]

    sums = lax.fori_loop(1, peers, receive, x_buf[0])
    inverse = 1.0 / jnp.sqrt(sums[0:1, :] / total + EPSILON)
    coef = inverse * inverse * inverse * (sums[1:2, :] / total)
    inv_full[...] = jnp.transpose(jnp.broadcast_to(inverse, (DH, rows)))
    coef_full[...] = jnp.transpose(jnp.broadcast_to(coef, (DH, rows)))

    def make_grads(h, carried):
        rate = rate_ref[h]
        reach = reach_in(rate)
        gain = gain_ref[pl.ds(h, 1), :]
        state = jnp.zeros((DH, DH), F32)
        factor = jnp.ones((8, DH), F32)
        for c in reversed(range(chunks)):
            a, inv = att[h, part(c), :], inv_full[part(c), :]
            n_out[part(c), cols(h)] = (a * inv * gain).astype(BF16)
            gained = gs[h, part(c), :].astype(F32) * gain
            grad = (inv * gained - a * coef_full[part(c), :]).astype(BF16)
            ga[h, part(c), :] = grad
            weighted = (qs[h, part(c), :].astype(F32) * (reach * in_mask[c])).astype(BF16)
            add = dot(weighted, grad, 0, 0)
            d_grad[h, c] = add
            keep = carry(rate, c)
            state = keep[0:1, :] * state + add
            factor = factor * keep
        put(1, 0, h, state, factor)
        scan_copy(1, 0, h).start()
        return carried

    lax.fori_loop(0, heads, make_grads, 0)

    def inner_grads(h, carried):
        rate = rate_ref[h]
        decay = jnp.exp(-rate * gap)
        reach = reach_in(rate)
        for c in range(chunks):
            grad = ga[h, part(c), :]
            d = (dot(grad, vs[h, part(c), :], 1, 1) * (decay * joined[c])).astype(BF16)
            gq = dot(d, ks[h, part(c), :], 1, 0)
            gq += (reach * in_mask[c]) * dot(grad, full_state[h, c], 1, 1)
            gq_out[part(c), cols(h)] = gq.astype(BF16)
            gkp[h, part(c), :] = dot(d, qs[h, part(c), :], 0, 0)
            gvp[h, part(c), :] = dot(weights[h, c], grad, 0, 0)
        for step in range(steps - 1):
            take(1, step, h, True)
        return carried

    lax.fori_loop(0, heads, inner_grads, 0)

    def finish_grads(h, carried):
        rate = rate_ref[h]
        state = take(1, steps - 1, h, False)
        out = reach_out(rate)
        for c in reversed(range(chunks)):
            small = state.astype(BF16)
            reach = out * out_mask[c]
            gk = gkp[h, part(c), :] + reach * dot(vs[h, part(c), :], small, 1, 1)
            gv = gvp[h, part(c), :] + reach * dot(ks[h, part(c), :], small, 1, 0)
            gk_out[part(c), cols(h)] = gk.astype(BF16)
            gv_out[part(c), cols(h)] = gv.astype(BF16)
            if c > 0:
                state = carry(rate, c)[0:1, :] * state + d_grad[h, c]
        return carried

    lax.fori_loop(0, heads, finish_grads, 0)

    def drain(h, carried):
        for which in range(2):
            for step in range(steps):
                scan_copy(which, step, h).wait_send()
        return carried

    lax.fori_loop(0, heads, drain, 0)

    def drain_swaps(k, c):
        swap_copy(k).wait_send()
        return c

    lax.fori_loop(1, peers, drain_swaps, 0)


def write_out(*refs):
    sems = refs[8]
    copies = [pltpu.make_async_copy(refs[i], refs[i + 4], sems.at[i]) for i in range(4)]
    for copy in copies:
        copy.start()
    for copy in copies:
        copy.wait()


def body(steps, peers, query_rows, key_rows, value_rows, decay_rate, starts, norm_gain, grad_out):
    rows, features = query_rows.shape
    heads = features // DH
    chunks = rows // CHUNK
    big = jax.ShapeDtypeStruct((rows, features), BF16)
    whole = pl.BlockSpec(memory_space=pltpu.HBM)
    inside = pl.BlockSpec(memory_space=pltpu.VMEM)

    def head_rows(dtype):
        return pltpu.VMEM((heads, rows, DH), dtype)

    dma = pltpu.SemaphoreType.DMA
    kept = pl.pallas_call(
        functools.partial(kernel, steps, peers, HEADS * DH),
        out_shape=(pltpu.VMEM((rows, features), BF16),) * 4,
        in_specs=[whole] * 4 + [pl.BlockSpec(memory_space=pltpu.SMEM), inside, inside],
        out_specs=(inside,) * 4,
        scratch_shapes=[head_rows(BF16)] * 4
        + [head_rows(F32), head_rows(BF16), pltpu.VMEM((heads, chunks, CHUNK, CHUNK), BF16)]
        + [head_rows(F32)] * 2
        + [
            pltpu.VMEM((chunks, CHUNK, CHUNK), F32),
            pltpu.VMEM((chunks, CHUNK, DH), F32),
            pltpu.VMEM((chunks, CHUNK, DH), F32),
            pltpu.VMEM((chunks, 8, DH), F32),
            pltpu.VMEM((heads, chunks, DH, DH), F32),
            pltpu.VMEM((heads, chunks, DH, DH), BF16),
            pltpu.VMEM((heads, chunks, DH, DH), F32),
            pltpu.VMEM((2, steps, heads, DH + 8, DH), F32),
            pltpu.VMEM((2, steps, heads, DH + 8, DH), F32),
            pltpu.VMEM((heads, DH + 8, DH), F32),
            pltpu.VMEM((rows, DH), F32),
            pltpu.VMEM((rows, DH), F32),
            pltpu.VMEM((rows, DH), F32),
            pltpu.VMEM((rows, DH), F32),
            pltpu.VMEM((peers, 2, rows), F32),
            dma((4, heads)),
            dma((2, steps, heads)),
            dma((2, steps, heads)),
            dma((peers,)),
            dma((peers,)),
        ],
        compiler_params=pltpu.CompilerParams(
            collective_id=0, has_side_effects=True, vmem_limit_bytes=55 * 1024 * 1024
        ),
    )(
        query_rows, key_rows, value_rows, grad_out, decay_rate,
        starts.reshape(1, rows), norm_gain.reshape(heads, DH),
    )
    return pl.pallas_call(
        write_out,
        out_shape=(big,) * 4,
        in_specs=[pl.BlockSpec(memory_space=pl.ANY)] * 4,
        out_specs=(whole,) * 4,
        scratch_shapes=[dma((4,))],
        compiler_params=pltpu.CompilerParams(vmem_limit_bytes=1024 * 1024),
    )(*kept)


def solution(mesh):
    steps = (mesh.shape["ctx"] - 1).bit_length()
    both = P("ctx", "head")
    return jax.shard_map(
        functools.partial(body, steps, mesh.shape["head"]),
        mesh=mesh,
        in_specs=(both, both, both, P("head"), P("ctx"), P("head"), both),
        out_specs=(both,) * 4,
        check_vma=False,
    )
```

```python
import functools

import jax
import jax.numpy as jnp
from jax import lax
from jax.experimental import pallas as pl
from jax.experimental.pallas import tpu as pltpu
from jax.sharding import PartitionSpec as P

HEADS = 64
DH = 128
CHUNK = 128
AHEAD = 2
AHEAD_GRADS = 3
EPSILON = 1e-06
MESH = pl.DeviceIdType.MESH
F32 = jnp.float32
BF16 = jnp.bfloat16


def dot(a, b, da, db):
    return lax.dot_general(a, b, (((da,), (db,)), ((), ())), preferred_element_type=F32)


def kernel(
    steps, peers, total,
    q_hbm, k_hbm, v_hbm, g_hbm, rate_ref, starts_ref, gain_ref,
    n_out, gq_out, gk_out, gv_out,
    qs, ks, vs, gs, att, ga, weights, gkp, gvp,
    joined, in_mask, out_mask, clear, d_state, full_state, d_grad,
    own, got, pre, sq_acc, cr_acc, inv_full, coef_full, x_buf,
    in_sem, s_send, s_recv, x_send, x_recv,
):
    heads, rows, _ = qs.shape
    chunks = rows // CHUNK
    ctx = lax.axis_index("ctx")
    me = lax.axis_index("head")

    def cols(h):
        return pl.ds(pl.multiple_of(h * DH, DH), DH)

    def load(i, h):
        hbm, buf = ((k_hbm, ks), (v_hbm, vs), (q_hbm, qs), (g_hbm, gs))[i]
        return pltpu.make_async_copy(hbm.at[:, cols(h)], buf.at[h], in_sem.at[i, h])

    def partner(step):
        size = 1 << step
        bit = (ctx // size) % 2
        return bit, ctx + size - 2 * size * bit

    def scan_copy(which, step, h):
        return pltpu.make_async_remote_copy(
            src_ref=own.at[which, step, h],
            dst_ref=got.at[which, step, h],
            send_sem=s_send.at[which, step, h],
            recv_sem=s_recv.at[which, step, h],
            device_id=(partner(step)[1], me),
            device_id_type=MESH,
        )

    def swap_copy(k):
        return pltpu.make_async_remote_copy(
            src_ref=x_buf.at[0],
            dst_ref=x_buf.at[k],
            send_sem=x_send.at[k],
            recv_sem=x_recv.at[k],
            device_id=(ctx, (me + k) % peers),
            device_id_type=MESH,
        )

    def start_loads(pair):
        def go(h, c):
            for i in pair:
                load(i, h).start()
            return c
        lax.fori_loop(0, heads, go, 0)

    start_loads((0, 1))
    start_loads((2, 3))

    barrier = pltpu.get_barrier_semaphore()
    for step in range(steps):
        pl.semaphore_signal(barrier, inc=1, device_id=(partner(step)[1], me), device_id_type=MESH)

    def greet(k, c):
        pl.semaphore_signal(
            barrier, inc=1, device_id=(ctx, (me + k) % peers), device_id_type=MESH
        )
        return c

    lax.fori_loop(1, peers, greet, 0)

    row_at = lax.broadcasted_iota(jnp.int32, (CHUNK, CHUNK), 0)
    col_at = lax.broadcasted_iota(jnp.int32, (CHUNK, CHUNK), 1)
    lower = row_at >= col_at
    ones_low = jnp.where(lower, 1.0, 0.0).astype(BF16)
    for c in range(chunks):
        flags = starts_ref[:, c * CHUNK:(c + 1) * CHUNK].astype(F32)
        wide = jnp.broadcast_to(flags, (DH, CHUNK)).astype(BF16)
        run_row = dot(wide, ones_low, 1, 1)[0:1, :]
        run_col = dot(ones_low, wide, 1, 1)
        count = jnp.sum(flags, axis=1, keepdims=True)
        both = jnp.concatenate([run_col] * (CHUNK // DH), axis=1)
        joined[c] = jnp.where(lower & (both == run_row), 1.0, 0.0)
        in_mask[c] = jnp.where(run_col == 0.0, 1.0, 0.0)
        out_mask[c] = jnp.where(run_col == count, 1.0, 0.0)
        clear[c] = jnp.broadcast_to(jnp.where(count == 0.0, 1.0, 0.0), (8, DH))
    sq_acc[...] = jnp.zeros_like(sq_acc)
    cr_acc[...] = jnp.zeros_like(cr_acc)

    place = lax.broadcasted_iota(jnp.int32, (CHUNK, DH), 0).astype(F32)
    gap = jnp.maximum(row_at - col_at, 0).astype(F32)

    def reach_in(rate):
        return jnp.exp(-rate * (place + 1.0))

    def reach_out(rate):
        return jnp.exp(-rate * (CHUNK - 1.0 - place))

    def carry(rate, c):
        return clear[c] * jnp.exp(jnp.full((8, DH), -rate * CHUNK, F32))

    def put(which, step, h, state, factor):
        own[which, step, h, 0:DH, :] = state
        own[which, step, h, DH:DH + 8, :] = factor

    def take(which, step, h, want_total):
        scan_copy(which, step, h).wait_recv()
        bit, _ = partner(step)
        ahead = (bit == 1) if which == 0 else (bit == 0)
        came, came_f = got[which, step, h, 0:DH, :], got[which, step, h, DH:DH + 8, :]
        if step == 0:
            state = jnp.where(ahead, came, 0.0)
            factor = jnp.where(ahead, came_f, 1.0)
        else:
            old, old_f = pre[h, 0:DH, :], pre[h, DH:DH + 8, :]
            state = jnp.where(ahead, old_f[0:1, :] * came + old, old)
            factor = jnp.where(ahead, old_f * came_f, old_f)
        if not want_total:
            return state
        pre[h, 0:DH, :] = state
        pre[h, DH:DH + 8, :] = factor
        mine, mine_f = own[which, step, h, 0:DH, :], own[which, step, h, DH:DH + 8, :]
        merged = jnp.where(ahead, mine_f[0:1, :] * came + mine, came_f[0:1, :] * mine + came)
        put(which, step + 1, h, merged, mine_f * came_f)
        scan_copy(which, step + 1, h).start()
        return None

    def part(c):
        return slice(c * CHUNK, (c + 1) * CHUNK)

    pl.semaphore_wait(barrier, steps + peers - 1)

    def make_states(h, carried):
        load(0, h).wait()
        load(1, h).wait()
        rate = rate_ref[h]
        out = reach_out(rate)
        state = jnp.zeros((DH, DH), F32)
        factor = jnp.ones((8, DH), F32)
        for c in range(chunks):
            weighted = (ks[h, part(c), :].astype(F32) * (out * out_mask[c])).astype(BF16)
            add = dot(weighted, vs[h, part(c), :], 0, 0)
            d_state[h, c] = add
            keep = carry(rate, c)
            state = keep[0:1, :] * state + add
            factor = factor * keep
        put(0, 0, h, state, factor)
        scan_copy(0, 0, h).start()
        return carried

    lax.fori_loop(0, heads, make_states, 0)

    def attend(h, carried):
        load(2, h).wait()
        load(3, h).wait()
        decay = jnp.exp(-rate_ref[h] * gap)
        def raw(c):
            return dot(qs[h, part(c), :], ks[h, part(c), :], 1, 1)

        ready = [raw(c) for c in range(min(AHEAD, chunks))]
        for c in range(chunks):
            scores = ready.pop(0)
            if c + AHEAD < chunks:
                ready.append(raw(c + AHEAD))
            w = (scores * (decay * joined[c])).astype(BF16)
            weights[h, c] = jnp.transpose(w)
            att[h, part(c), :] = dot(w, vs[h, part(c), :], 1, 0)
        for step in range(steps - 1):
            take(0, step, h, True)
        return carried

    lax.fori_loop(0, heads, attend, 0)

    def finish_attend(h, carried):
        rate = rate_ref[h]
        state = take(0, steps - 1, h, False)
        reach = reach_in(rate)
        gain = gain_ref[pl.ds(h, 1), :]
        for c in range(chunks):
            small = state.astype(BF16)
            full_state[h, c] = small
            a = att[h, part(c), :] + (reach * in_mask[c]) * dot(qs[h, part(c), :], small, 1, 0)
            att[h, part(c), :] = a
            sq_acc[part(c), :] += a * a
            cr_acc[part(c), :] += gs[h, part(c), :].astype(F32) * gain * a
            if c < chunks - 1:
                state = carry(rate, c)[0:1, :] * state + d_state[h, c]
        return carried

    lax.fori_loop(0, heads, finish_attend, 0)

    x_buf[0, 0:1, :] = jnp.sum(jnp.transpose(sq_acc[...]), axis=0, keepdims=True)
    x_buf[0, 1:2, :] = jnp.sum(jnp.transpose(cr_acc[...]), axis=0, keepdims=True)

    def send(k, c):
        swap_copy(k).start()
        return c

    lax.fori_loop(1, peers, send, 0)

    def receive(k, c):
        swap_copy(k).wait_recv()
        return c + x_buf[k]

    sums = lax.fori_loop(1, peers, receive, x_buf[0])
    inverse = 1.0 / jnp.sqrt(sums[0:1, :] / total + EPSILON)
    coef = inverse * inverse * inverse * (sums[1:2, :] / total)
    inv_full[...] = jnp.transpose(jnp.broadcast_to(inverse, (DH, rows)))
    coef_full[...] = jnp.transpose(jnp.broadcast_to(coef, (DH, rows)))

    def make_grads(h, carried):
        rate = rate_ref[h]
        reach = reach_in(rate)
        gain = gain_ref[pl.ds(h, 1), :]
        state = jnp.zeros((DH, DH), F32)
        factor = jnp.ones((8, DH), F32)
        for c in reversed(range(chunks)):
            a, inv = att[h, part(c), :], inv_full[part(c), :]
            n_out[part(c), cols(h)] = (a * inv * gain).astype(BF16)
            gained = gs[h, part(c), :].astype(F32) * gain
            grad = (inv * gained - a * coef_full[part(c), :]).astype(BF16)
            ga[h, part(c), :] = grad
            weighted = (qs[h, part(c), :].astype(F32) * (reach * in_mask[c])).astype(BF16)
            add = dot(weighted, grad, 0, 0)
            d_grad[h, c] = add
            keep = carry(rate, c)
            state = keep[0:1, :] * state + add
            factor = factor * keep
        put(1, 0, h, state, factor)
        scan_copy(1, 0, h).start()
        return carried

    lax.fori_loop(0, heads, make_grads, 0)

    def inner_grads(h, carried):
        rate = rate_ref[h]
        decay = jnp.exp(-rate * gap)
        reach = reach_in(rate)
        def raw(c):
            grad = ga[h, part(c), :]
            return dot(grad, vs[h, part(c), :], 1, 1), dot(grad, full_state[h, c], 1, 1)

        ready = [raw(c) for c in range(min(AHEAD_GRADS, chunks))]
        for c in range(chunks):
            wide, far = ready.pop(0)
            if c + AHEAD_GRADS < chunks:
                ready.append(raw(c + AHEAD_GRADS))
            gvp[h, part(c), :] = dot(weights[h, c], ga[h, part(c), :], 1, 0)
            d = (wide * (decay * joined[c])).astype(BF16)
            gq = dot(d, ks[h, part(c), :], 1, 0) + (reach * in_mask[c]) * far
            gq_out[part(c), cols(h)] = gq.astype(BF16)
            gkp[h, part(c), :] = dot(d, qs[h, part(c), :], 0, 0)
        for step in range(steps - 1):
            take(1, step, h, True)
        return carried

    lax.fori_loop(0, heads, inner_grads, 0)

    def finish_grads(h, carried):
        rate = rate_ref[h]
        state = take(1, steps - 1, h, False)
        out = reach_out(rate)
        for c in reversed(range(chunks)):
            small = state.astype(BF16)
            reach = out * out_mask[c]
            gk = gkp[h, part(c), :] + reach * dot(vs[h, part(c), :], small, 1, 1)
            gv = gvp[h, part(c), :] + reach * dot(ks[h, part(c), :], small, 1, 0)
            gk_out[part(c), cols(h)] = gk.astype(BF16)
            gv_out[part(c), cols(h)] = gv.astype(BF16)
            if c > 0:
                state = carry(rate, c)[0:1, :] * state + d_grad[h, c]
        return carried

    lax.fori_loop(0, heads, finish_grads, 0)

    def drain(h, carried):
        for which in range(2):
            for step in range(steps):
                scan_copy(which, step, h).wait_send()
        return carried

    lax.fori_loop(0, heads, drain, 0)

    def drain_swaps(k, c):
        swap_copy(k).wait_send()
        return c

    lax.fori_loop(1, peers, drain_swaps, 0)


def write_out(*refs):
    sems = refs[8]
    copies = [pltpu.make_async_copy(refs[i], refs[i + 4], sems.at[i]) for i in range(4)]
    for copy in copies:
        copy.start()
    for copy in copies:
        copy.wait()


def body(steps, peers, query_rows, key_rows, value_rows, decay_rate, starts, norm_gain, grad_out):
    rows, features = query_rows.shape
    heads = features // DH
    chunks = rows // CHUNK
    big = jax.ShapeDtypeStruct((rows, features), BF16)
    whole = pl.BlockSpec(memory_space=pltpu.HBM)
    inside = pl.BlockSpec(memory_space=pltpu.VMEM)

    def head_rows(dtype):
        return pltpu.VMEM((heads, rows, DH), dtype)

    dma = pltpu.SemaphoreType.DMA
    kept = pl.pallas_call(
        functools.partial(kernel, steps, peers, HEADS * DH),
        out_shape=(pltpu.VMEM((rows, features), BF16),) * 4,
        in_specs=[whole] * 4 + [pl.BlockSpec(memory_space=pltpu.SMEM), inside, inside],
        out_specs=(inside,) * 4,
        scratch_shapes=[head_rows(BF16)] * 4
        + [head_rows(F32), head_rows(BF16), pltpu.VMEM((heads, chunks, CHUNK, CHUNK), BF16)]
        + [head_rows(F32)] * 2
        + [
            pltpu.VMEM((chunks, CHUNK, CHUNK), F32),
            pltpu.VMEM((chunks, CHUNK, DH), F32),
            pltpu.VMEM((chunks, CHUNK, DH), F32),
            pltpu.VMEM((chunks, 8, DH), F32),
            pltpu.VMEM((heads, chunks, DH, DH), F32),
            pltpu.VMEM((heads, chunks, DH, DH), BF16),
            pltpu.VMEM((heads, chunks, DH, DH), F32),
            pltpu.VMEM((2, steps, heads, DH + 8, DH), F32),
            pltpu.VMEM((2, steps, heads, DH + 8, DH), F32),
            pltpu.VMEM((heads, DH + 8, DH), F32),
            pltpu.VMEM((rows, DH), F32),
            pltpu.VMEM((rows, DH), F32),
            pltpu.VMEM((rows, DH), F32),
            pltpu.VMEM((rows, DH), F32),
            pltpu.VMEM((peers, 2, rows), F32),
            dma((4, heads)),
            dma((2, steps, heads)),
            dma((2, steps, heads)),
            dma((peers,)),
            dma((peers,)),
        ],
        compiler_params=pltpu.CompilerParams(
            collective_id=0, has_side_effects=True, vmem_limit_bytes=55 * 1024 * 1024
        ),
    )(
        query_rows, key_rows, value_rows, grad_out, decay_rate,
        starts.reshape(1, rows), norm_gain.reshape(heads, DH),
    )
    return pl.pallas_call(
        write_out,
        out_shape=(big,) * 4,
        in_specs=[pl.BlockSpec(memory_space=pl.ANY)] * 4,
        out_specs=(whole,) * 4,
        scratch_shapes=[dma((4,))],
        compiler_params=pltpu.CompilerParams(vmem_limit_bytes=1024 * 1024),
    )(*kept)


def solution(mesh):
    steps = (mesh.shape["ctx"] - 1).bit_length()
    both = P("ctx", "head")
    return jax.shard_map(
        functools.partial(body, steps, mesh.shape["head"]),
        mesh=mesh,
        in_specs=(both, both, both, P("head"), P("ctx"), P("head"), both),
        out_specs=(both,) * 4,
        check_vma=False,
    )
```
